32 devices in a mesh: gx: 8 (over z, y), gy: 4 (over x, core).
Axes of the slice: x: 2, y: 2, z: 4, core: 2. Of those that a mesh axis runs over, the one named last changes fastest.
Arguments:
- right_side: float32 [64, 128, 128], P('gy', 'gx'), may hold values from -6 to 9
- diagonal: float32 [64, 128, 128], P('gy', 'gx'), may hold values from 0.02 to 0.5
- horizontal: float32 [64, 128, 128], P('gy', 'gx'), may hold values from 0.1 to 1
- vertical: float32 [128], replicated, may hold values from 0.2 to 2
- precond: float32 [2, 128, 128], replicated, may hold values from -4 to 4
- edge_rows: int32 [2, 64], replicated, may hold values from 0 to 63, as said below
Outputs:
- solution_field: float32 [64, 128, 128], P('gy', 'gx')
- residual: float32 [64, 128, 128], P('gy', 'gx')
- residual_sq: float32 [3], replicated
The draws below stay inside these ranges and needn't reach their ends.
Inputs may be any that keep to these rules, and one draw needn't show every extreme that they name: Each row of edge_rows lists every number 0 to 63 exactly once.
All inputs are finite; a program needn't handle non-finite values.
Results may differ from the reference program's by a relative error of at most 0.00014.
Values sent between devices are 32-bit elements; how exact they have to be, the bound alone decides.
No kernel may reach another device: no remote copies, remote signals or barrier semaphores. Data moves between devices by JAX's collectives and lax.ppermute only.
A program may use at most 64 MiB of HBM per device.

```python
import math
import jax
import jax.numpy as jnp
from jax import lax

LEV = 128
ITERS = 3
NX = 128
NY = 64


def draw_right_side(key, part):
    base = jnp.clip(jax.random.normal(key, (NY, NX, LEV), jnp.float32), -6.0, 6.0)
    return base


def draw_precond(key, part):
    keys = jax.random.split(key, 3)
    extra = jax.random.uniform(keys[0], (2, LEV), jnp.float32, 0.3, 1.0)
    couple = jax.random.uniform(keys[1], (2, LEV - 1), jnp.float32, 0.5, 2.0)
    padded = jnp.pad(couple, ((0, 0), (1, 1)))
    main = extra + padded[:, :-1] + padded[:, 1:]
    couple_row = jnp.pad(couple, ((0, 0), (0, 1)))
    upper = jnp.eye(LEV, k=1, dtype=jnp.float32)
    lower = jnp.eye(LEV, k=-1, dtype=jnp.float32)
    eye = jnp.eye(LEV, dtype=jnp.float32)
    tri = main[:, :, None] * eye[None] - couple_row[:, :, None] * upper[None] - couple_row[:, None, :] * lower[None]
    inverse = jnp.linalg.inv(tri)
    size = jnp.mean(jnp.abs(jnp.diagonal(inverse, axis1=1, axis2=2)), axis=1)
    noise = jax.random.normal(keys[2], (2, LEV, LEV), jnp.float32)
    return inverse + 0.05 * size[:, None, None] * noise


def draw_edge_rows(key, part):
    first = jax.random.permutation(jax.random.fold_in(key, 11), NY).astype(jnp.int32)
    second = jax.random.permutation(jax.random.fold_in(key, 23), NY).astype(jnp.int32)
    return jnp.stack([first, second]).astype(jnp.int32)


def block_scale(rng, dims, pieces, least, largest):
    loudness = 1.0
    for dim, parts in pieces:
        draws = jax.random.uniform(jax.random.fold_in(jax.random.fold_in(rng, 6), dim), (parts,), jnp.float32, least / len(pieces), largest / len(pieces))
        loudness = loudness * jnp.repeat(jnp.exp(draws), dims[dim] // parts).reshape((-1,) + (1,) * (len(dims) - 1 - dim))
    return loudness


def setup_inputs(seed: int = 0) -> dict:
    seeds = jax.random.split(jax.random.key(seed), 7)
    right_side = draw_right_side(jax.random.fold_in(seeds[6], 71), 0)
    diagonal = jnp.clip(jnp.exp(math.log(0.5) - 3.218876 * jax.random.uniform(seeds[1], (NY, NX, LEV), jnp.float32) ** block_scale(seeds[1], (NY, NX, LEV), ((0, 4), (1, 8)), -0.2, 0.2)), 0.02, 0.5)
    horizontal = jnp.clip(jnp.exp(math.log(1.0) - 2.3025851 * jax.random.uniform(seeds[2], (NY, NX, LEV), jnp.float32) ** block_scale(seeds[2], (NY, NX, LEV), ((0, 4), (1, 8)), -0.2, 0.2)), 0.1, 1.0)
    vertical = jnp.clip(jnp.exp(jax.random.uniform(seeds[3], (LEV,), jnp.float32, math.log(0.2), math.log(2.0))), 0.2, 2.0)
    precond = draw_precond(jax.random.fold_in(seeds[6], 71), 0)
    edge_rows = draw_edge_rows(jax.random.fold_in(seeds[6], 71), 0)
    return dict(right_side=right_side, diagonal=diagonal, horizontal=horizontal, vertical=vertical, precond=precond, edge_rows=edge_rows)


def operate(field, diagonal, horizontal, vertical, edge_rows):
    width = field.shape[1]
    half = width // 2
    east = jnp.roll(field, -1, 1)
    east = east.at[:, half - 1].set(field[edge_rows[0], half]).at[:, width - 1].set(field[edge_rows[1], 0])
    west = jnp.roll(field, 1, 1)
    west = west.at[:, half].set(field[edge_rows[0], half - 1]).at[:, 0].set(field[edge_rows[1], width - 1])
    tall = jnp.pad(field, ((1, 1), (0, 0), (0, 0)))
    flat = jnp.pad(field, ((0, 0), (0, 0), (1, 1)))
    beside = east + west + tall[2:] + tall[:-2]
    column = flat[:, :, 2:] + flat[:, :, :-2]
    return diagonal * field + horizontal * (4.0 * field - beside) + vertical * (2.0 * field - column)

def precondition(field, precond):
    half = field.shape[1] // 2
    left = jnp.einsum('yxl,kl->yxk', field[:, :half], precond[0], precision=lax.Precision.HIGHEST)
    right = jnp.einsum('yxl,kl->yxk', field[:, half:], precond[1], precision=lax.Precision.HIGHEST)
    return jnp.concatenate([left, right], 1)

def reference(right_side, diagonal, horizontal, vertical, precond, edge_rows):
    total_cells = float(right_side.size)

    def inner(left, right):
        return jnp.sum(left * right) / total_cells
    solution_field = jnp.zeros_like(right_side)
    residual = right_side
    directions = []
    images = []
    norms = []
    for step in range(ITERS):
        pre = precondition(residual, precond)
        image = operate(pre, diagonal, horizontal, vertical, edge_rows)
        coeffs = [inner(image, older) for older in images]
        for number in range(len(images)):
            pre = pre - coeffs[number] * directions[number]
            image = image - coeffs[number] * images[number]
        scale = 1.0 / jnp.sqrt(inner(image, image))
        direction = pre * scale
        image = image * scale
        alpha = inner(residual, image)
        solution_field = solution_field + alpha * direction
        residual = residual - alpha * image
        norms.append(inner(residual, residual))
        directions.append(direction)
        images.append(image)
    return (solution_field, residual, jnp.stack(norms))
```

```python
import functools

import jax
import jax.numpy as jnp
from jax import lax
from jax.experimental import pallas as pl
from jax.experimental.pallas import tpu as pltpu
from jax.sharding import PartitionSpec as P

HI = lax.Precision.HIGHEST
VM = pl.BlockSpec(memory_space=pltpu.VMEM)
SM = pl.BlockSpec(memory_space=pltpu.SMEM)


def krylov_kernel(tbl, meta, r_ref, d_ref, h_ref, before, after, ag, vert_ref, pc_ref,
                  zs_ref, ws_ref, gram_ref, n0_ref, o0_ref, gath_ref, cross_ref, halo_ref):
    rows, cols, lev = r_ref.shape
    n_gy = ag.shape[0]
    high = rows * n_gy
    first = meta[0]
    vert = vert_ref[...]
    m_own = pc_ref[meta[1]]
    m_side = (pc_ref[meta[2]], pc_ref[meta[3]])

    def mul(v, m):
        shape = v.shape
        out = lax.dot_general(v.reshape(-1, lev), m, (((1,), (1,)), ((), ())), precision=HI,
                              preferred_element_type=jnp.float32)
        return out.reshape(shape)

    def column_term(z):
        axis = z.ndim - 1
        lane = lax.broadcasted_iota(jnp.int32, z.shape, axis)
        up = jnp.where(lane == lev - 1, 0.0, pltpu.roll(z, lev - 1, axis))
        down = jnp.where(lane == 0, 0.0, pltpu.roll(z, 1, axis))
        return vert * (2.0 * z - up - down)

    def strip_apply(z, d, h, east, west):
        row = lax.broadcasted_iota(jnp.int32, z.shape, 0)
        north = jnp.where(row == high - 1, 0.0, pltpu.roll(z, high - 1, 0))
        south = jnp.where(row == 0, 0.0, pltpu.roll(z, 1, 0))
        return d * z + h * (4.0 * z - east - west - north - south) + column_term(z)

    def block_apply(z, d, h, halo_e, halo_w):
        mid = z[1:-1]
        col = lax.broadcasted_iota(jnp.int32, mid.shape, 1)
        east = jnp.where(col == cols - 1, halo_e, pltpu.roll(mid, cols - 1, 1))
        west = jnp.where(col == 0, halo_w, pltpu.roll(mid, 1, 1))
        return d * mid + h * (4.0 * mid - east - west - z[2:] - z[:-2]) + column_term(mid)

    def strip(c):
        return jnp.concatenate([ag[g, c] for g in range(n_gy)], 0)

    def gather_rows(side):
        def body(y, _):
            gath_ref[side, pl.ds(y, 1), :] = n0_ref[side, pl.ds(tbl[side, y], 1), :]
            return 0
        lax.fori_loop(0, high, body, 0, unroll=16)

    def gather_own(side):
        def body(y, _):
            cross_ref[side, pl.ds(y, 1), :] = o0_ref[side, pl.ds(tbl[side, y], 1), :]
            return 0
        lax.fori_loop(0, high, body, 0, unroll=16)

    def halo_rows(side, depth):
        for k in range(rows + 2 * depth):
            y = jnp.clip(first - depth + k, 0, high - 1)
            halo_ref[side, k] = n0_ref[side, pl.ds(tbl[side, y], 1), :]
        return halo_ref[side, : rows + 2 * depth]

    r = r_ref[...]
    block = jnp.concatenate([before[0:3], r, after[0:3]], 0)
    d = jnp.concatenate([before[3:5], d_ref[...], after[3:5]], 0)
    h = jnp.concatenate([before[5:7], h_ref[...], after[5:7]], 0)

    own = mul(jnp.stack([strip(c) for c in (0, 1, 4, 5)], 0), m_own)
    o0 = [own[0], own[2]]
    o1 = [own[1], own[3]]
    near = [mul(jnp.stack([strip(8 + 7 * s + c) for c in range(3)], 0), m_side[s]) for s in range(2)]
    for s in range(2):
        n0_ref[s] = near[s][0]
        o0_ref[s] = o0[s]
    z = mul(block, m_own)
    zs_ref[0] = z[3:-3]
    for s in range(2):
        gather_rows(s)
        gather_own(s)
    w_o0 = []
    w_near = []
    for s in range(2):
        base = 8 + 7 * s
        w_o0.append(strip_apply(o0[s], strip(4 * s + 2), strip(4 * s + 3), gath_ref[s], o1[s]))
        a = strip_apply(near[s][0], strip(base + 3), strip(base + 5), near[s][1], cross_ref[s])
        b = strip_apply(near[s][1], strip(base + 4), strip(base + 6), near[s][2], near[s][0])
        w_near.append(jnp.stack([a, b], 0))
    w = block_apply(z, d, h, halo_rows(0, 2), halo_rows(1, 2))
    w0 = w[2:-2]
    ws_ref[0] = w0

    own = mul(jnp.stack(w_o0, 0), m_own)
    near = [mul(w_near[s], m_side[s]) for s in range(2)]
    for s in range(2):
        n0_ref[s] = near[s][0]
        o0_ref[s] = own[s]
    z = mul(w, m_own)
    zs_ref[1] = z[2:-2]
    for s in range(2):
        gather_own(s)
    w_near = []
    for s in range(2):
        base = 8 + 7 * s
        w_near.append(strip_apply(near[s][0], strip(base + 3), strip(base + 5), near[s][1], cross_ref[s]))
    w = block_apply(z, d[1:-1], h[1:-1], halo_rows(0, 1), halo_rows(1, 1))
    w1 = w[1:-1]
    ws_ref[1] = w1

    for s in range(2):
        n0_ref[s] = mul(w_near[s], m_side[s])
    z = mul(w, m_own)
    zs_ref[2] = z[1:-1]
    w2 = block_apply(z, d[2:-2], h[2:-2], halo_rows(0, 0), halo_rows(1, 0))
    ws_ref[2] = w2

    vectors = (r, w0, w1, w2)
    lane = lax.broadcasted_iota(jnp.int32, (1, lev), 1)
    row = jnp.zeros((1, lev), jnp.float32)
    count = 0
    for i in range(4):
        for j in range(i, 4):
            part = jnp.sum(vectors[i] * vectors[j], axis=0)
            part = jnp.sum(jnp.sum(part, axis=0, keepdims=True), axis=1, keepdims=True)
            row = jnp.where(lane == count, part, row)
            count += 1
    gram_ref[...] = jnp.broadcast_to(row[None], gram_ref.shape)


def combine_kernel(parts, r_ref, zs_ref, ws_ref, x_ref, res_ref, norm_ref, *, cells):
    total = jnp.sum(parts[...], axis=0) * (1.0 / cells)
    gram = {}
    count = 0
    for i in range(4):
        for j in range(i, 4):
            gram[i, j] = gram[j, i] = total[:, count : count + 1]
            count += 1

    def inner(a, b):
        out = None
        for i in a:
            for j in b:
                term = a[i] * b[j] * gram[i, j]
                out = term if out is None else out + term
        return out

    def axpy(a, c, b):
        out = dict(a)
        for i in b:
            out[i] = out[i] - c * b[i] if i in out else -c * b[i]
        return out

    one = jnp.ones((1, 1), jnp.float32)
    field = {}
    res = {0: one}
    directions = []
    images = []
    for step in range(3):
        pre = dict(res)
        image = {i + 1: res[i] for i in res}
        coeffs = [inner(image, older) for older in images]
        for c, p, q in zip(coeffs, directions, images):
            pre = axpy(pre, c, p)
            image = axpy(image, c, q)
        scale = 1.0 / jnp.sqrt(inner(image, image))
        pre = {i: pre[i] * scale for i in pre}
        image = {i: image[i] * scale for i in image}
        alpha = inner(res, image)
        field = axpy(field, -alpha, pre)
        res = axpy(res, alpha, image)
        norm_ref[step] = inner(res, res)[0, 0]
        directions.append(pre)
        images.append(image)
    x_ref[...] = field[0] * zs_ref[0] + field[1] * zs_ref[1] + field[2] * zs_ref[2]
    res_ref[...] = res[0] * r_ref[...] + res[1] * ws_ref[0] + res[2] * ws_ref[1] + res[3] * ws_ref[2]


def on_device(right_side, diagonal, horizontal, vertical, precond, edge_rows):
    rows, cols, levels = right_side.shape
    n_gx = lax.axis_size("gx")
    n_gy = lax.axis_size("gy")
    n_dev = n_gx * n_gy
    high = rows * n_gy
    cells = float(rows * cols * levels * n_dev)
    gx = lax.axis_index("gx")
    gy = lax.axis_index("gy")
    half = n_gx // 2
    side_panel = lambda c: (c % n_gx) // half
    own_panel = side_panel(gx)
    east_panel = side_panel(gx + 1)
    west_panel = side_panel(gx + n_gx - 1)
    straight = jnp.arange(high, dtype=jnp.int32)
    east_edge = jnp.where(gx == half - 1, edge_rows[0], edge_rows[1])
    west_edge = jnp.where(gx == half, edge_rows[0], edge_rows[1])
    tbl = jnp.stack([
        jnp.where(east_panel != own_panel, east_edge, straight),
        jnp.where(west_panel != own_panel, west_edge, straight),
    ])
    meta = jnp.stack([gy * rows, own_panel, east_panel, west_panel]).astype(jnp.int32)

    def pack(order):
        arrays = [right_side[:, order[k]] for k in range(3)]
        arrays += [diagonal[:, order[k]] for k in range(2)]
        arrays += [horizontal[:, order[k]] for k in range(2)]
        return jnp.stack(arrays, 0)

    east_pack = pack((cols - 1, cols - 2, cols - 3))
    west_pack = pack((0, 1, 2))
    ring = [(i, (i + 1) % n_gx) for i in range(n_gx)]
    back = [(j, i) for i, j in ring]
    from_east = lax.ppermute(west_pack, "gx", back)
    from_west = lax.ppermute(east_pack, "gx", ring)
    line = [(i, i + 1) for i in range(n_gy - 1)]
    last = jnp.concatenate([right_side[-3:], diagonal[-2:], horizontal[-2:]], 0)
    initial = jnp.concatenate([right_side[:3], diagonal[:2], horizontal[:2]], 0)
    before = lax.ppermute(last, "gy", line)
    after = lax.ppermute(initial, "gy", [(j, i) for i, j in line])
    trim = lambda p: jnp.concatenate([p[0:2], p[3:4], p[5:6]], 0)
    strips = jnp.concatenate([trim(east_pack), trim(west_pack), from_east, from_west], 0)
    ag = lax.all_gather(strips, "gy")

    f32 = jnp.float32
    zs, ws, gram = pl.pallas_call(
        krylov_kernel,
        out_shape=(
            jax.ShapeDtypeStruct((3, rows, cols, levels), f32),
            jax.ShapeDtypeStruct((3, rows, cols, levels), f32),
            jax.ShapeDtypeStruct((n_dev, 1, levels), f32),
        ),
        in_specs=[SM, SM] + [VM] * 8,
        out_specs=(VM, VM, VM),
        scratch_shapes=[pltpu.VMEM((2, high, levels), f32)] * 4
        + [pltpu.VMEM((2, rows + 4, 1, levels), f32)],
        name="krylov",
    )(tbl, meta, right_side, diagonal, horizontal, before, after, ag, vertical[None], precond)

    parts = lax.all_to_all(gram, ("gx", "gy"), 0, 0)
    return pl.pallas_call(
        functools.partial(combine_kernel, cells=cells),
        out_shape=(
            jax.ShapeDtypeStruct((rows, cols, levels), f32),
            jax.ShapeDtypeStruct((rows, cols, levels), f32),
            jax.ShapeDtypeStruct((3,), f32),
        ),
        in_specs=[VM] * 4,
        out_specs=(VM, VM, SM),
        name="combine",
    )(parts, right_side, zs, ws)


def solution(mesh):
    in_specs = (P("gy", "gx", None), P("gy", "gx", None), P("gy", "gx", None), P(), P(), P())
    out_specs = (P("gy", "gx", None), P("gy", "gx", None), P())
    return jax.shard_map(
        on_device, mesh=mesh, in_specs=in_specs, out_specs=out_specs, check_vma=False
    )
```

```python
import functools

import jax
import jax.numpy as jnp
from jax import lax
from jax.experimental import pallas as pl
from jax.experimental.pallas import tpu as pltpu
from jax.sharding import PartitionSpec as P

PAD = 8
HI = lax.Precision.HIGHEST
VM = pl.BlockSpec(memory_space=pltpu.VMEM)
SM = pl.BlockSpec(memory_space=pltpu.SMEM)


def position(n_gx):
    gx = lax.axis_index("gx")
    half = n_gx // 2
    east = (gx == half - 1) | (gx == n_gx - 1)
    west = (gx == half) | (gx == 0)
    return gx, half, east, west


def pack_kernel(r_ref, d_ref, h_ref, east_ref, west_ref):
    cols = r_ref.shape[1]
    slot = 0
    for ref, depth in ((r_ref, 3), (d_ref, 2), (h_ref, 2)):
        for k in range(depth):
            east_ref[slot] = ref[:, cols - 1 - k, :]
            west_ref[slot] = ref[:, k, :]
            slot += 1


def widen_kernel(r_ref, d_ref, h_ref, east_own, west_own, east_ref, west_ref,
                 rw_ref, dw_ref, hw_ref, last_ref, first_ref, strip_ref, *, n_gx):
    rows, cols, lev = r_ref.shape
    _, _, seam_east, _ = position(n_gx)
    slot = 0
    for ref, wide, depth in ((r_ref, rw_ref, 3), (d_ref, dw_ref, 2), (h_ref, hw_ref, 2)):
        wide[:, :cols, :] = ref[...]
        wide[:, cols:, :] = jnp.zeros((rows, PAD, lev), jnp.float32)
        for k in range(depth):
            wide[:, cols + k, :] = east_ref[slot + k]
            wide[:, cols + PAD - 1 - k, :] = west_ref[slot + k]
        last_ref[slot : slot + depth] = wide[rows - depth :]
        first_ref[slot : slot + depth] = wide[:depth]
        slot += depth
    for place, k in enumerate((0, 1, 3, 5)):
        strip_ref[place] = jnp.where(seam_east, east_own[k], west_own[k])
    for k in range(7):
        strip_ref[4 + k] = jnp.where(seam_east, east_ref[k], west_ref[k])


def krylov_kernel(edges, rw_ref, dw_ref, hw_ref, before, after, ag, vert_ref, pc_ref,
                  zs_ref, ws_ref, gram_ref, n0_ref, o0_ref, gath_ref, cross_ref, halo_ref, *, n_gx):
    rows, wide, lev = rw_ref.shape
    cols = wide - PAD
    n_gy = ag.shape[0]
    high = rows * n_gy
    first = lax.axis_index("gy") * rows
    gx, half, seam_east, seam_west = position(n_gx)
    table = jnp.where((gx == half - 1) | (gx == half), 0, 1)
    seam_col = jnp.where(seam_east, cols, jnp.where(seam_west, wide - 1, -1))
    panel = gx // half
    vert = vert_ref[...]
    m_own = pc_ref[panel]
    m_near = pc_ref[1 - panel]

    def mul(v, m):
        shape = v.shape
        out = lax.dot_general(v.reshape(-1, lev), m, (((1,), (1,)), ((), ())), precision=HI,
                              preferred_element_type=jnp.float32)
        return out.reshape(shape)

    def column_term(z):
        axis = z.ndim - 1
        lane = lax.broadcasted_iota(jnp.int32, z.shape, axis)
        up = jnp.where(lane == lev - 1, 0.0, pltpu.roll(z, lev - 1, axis))
        down = jnp.where(lane == 0, 0.0, pltpu.roll(z, 1, axis))
        return vert * (2.0 * z - up - down)

    def strip_apply(z, d, h, east, west):
        row = lax.broadcasted_iota(jnp.int32, z.shape, 0)
        north = jnp.where(row == high - 1, 0.0, pltpu.roll(z, high - 1, 0))
        south = jnp.where(row == 0, 0.0, pltpu.roll(z, 1, 0))
        return d * z + h * (4.0 * z - east - west - north - south) + column_term(z)

    def block_apply(z, d, h, depth):
        for k in range(rows + 2 * depth):
            y = jnp.clip(first - depth + k, 0, high - 1)
            halo_ref[k] = n0_ref[pl.ds(edges[table, y], 1), :]
        mid = z[1:-1]
        col = lax.broadcasted_iota(jnp.int32, mid.shape, 1)
        mid = jnp.where(col == seam_col, halo_ref[: rows + 2 * depth], mid)
        beside = pltpu.roll(mid, wide - 1, 1) + pltpu.roll(mid, 1, 1) + z[2:] + z[:-2]
        return d * mid + h * (4.0 * mid - beside) + column_term(mid)

    def strip(c):
        return jnp.concatenate([ag[g, c] for g in range(n_gy)], 0)

    def gather(source, target):
        def body(y, _):
            target[pl.ds(y, 1), :] = source[pl.ds(edges[table, y], 1), :]
            return 0
        lax.fori_loop(0, high, body, 0, unroll=16)

    block = jnp.concatenate([before[0:3], rw_ref[...], after[0:3]], 0)
    d = jnp.concatenate([before[3:5], dw_ref[...], after[3:5]], 0)
    h = jnp.concatenate([before[5:7], hw_ref[...], after[5:7]], 0)

    own = mul(jnp.stack([strip(0), strip(1)], 0), m_own)
    near = mul(jnp.stack([strip(4), strip(5), strip(6)], 0), m_near)
    n0_ref[...] = near[0]
    o0_ref[...] = own[0]
    gather(n0_ref, gath_ref)
    gather(o0_ref, cross_ref)
    z = mul(block, m_own)
    zs_ref[0] = z[3:-3, :cols]
    w_o0 = strip_apply(own[0], strip(2), strip(3), gath_ref[...], own[1])
    w_n0 = strip_apply(near[0], strip(7), strip(9), near[1], cross_ref[...])
    w_n1 = strip_apply(near[1], strip(8), strip(10), near[2], near[0])
    w = block_apply(z, d, h, 2)
    w0 = w[2:-2, :cols]
    ws_ref[0] = w0

    o0_ref[...] = mul(w_o0, m_own)
    near = mul(jnp.stack([w_n0, w_n1], 0), m_near)
    n0_ref[...] = near[0]
    gather(o0_ref, cross_ref)
    z = mul(w, m_own)
    zs_ref[1] = z[2:-2, :cols]
    w_n0 = strip_apply(near[0], strip(7), strip(9), near[1], cross_ref[...])
    w = block_apply(z, d[1:-1], h[1:-1], 1)
    w1 = w[1:-1, :cols]
    ws_ref[1] = w1

    n0_ref[...] = mul(w_n0, m_near)
    z = mul(w, m_own)
    zs_ref[2] = z[1:-1, :cols]
    w2 = block_apply(z, d[2:-2], h[2:-2], 0)[:, :cols]
    ws_ref[2] = w2

    vectors = (rw_ref[:, :cols, :], w0, w1, w2)
    lane = lax.broadcasted_iota(jnp.int32, (1, lev), 1)
    row = jnp.zeros((1, lev), jnp.float32)
    count = 0
    for i in range(4):
        for j in range(i, 4):
            part = jnp.sum(vectors[i] * vectors[j], axis=0)
            part = jnp.sum(jnp.sum(part, axis=0, keepdims=True), axis=1, keepdims=True)
            row = jnp.where(lane == count, part, row)
            count += 1
    gram_ref[...] = jnp.broadcast_to(row[None], gram_ref.shape)


def combine_kernel(parts, r_ref, zs_ref, ws_ref, x_ref, res_ref, norm_ref, *, cells):
    total = jnp.sum(parts[...], axis=0) * (1.0 / cells)
    gram = {}
    count = 0
    for i in range(4):
        for j in range(i, 4):
            gram[i, j] = gram[j, i] = total[:, count : count + 1]
            count += 1

    def inner(a, b):
        out = None
        for i in a:
            for j in b:
                term = a[i] * b[j] * gram[i, j]
                out = term if out is None else out + term
        return out

    def axpy(a, c, b):
        out = dict(a)
        for i in b:
            out[i] = out[i] - c * b[i] if i in out else -c * b[i]
        return out

    one = jnp.ones((1, 1), jnp.float32)
    field = {}
    res = {0: one}
    directions = []
    images = []
    for step in range(3):
        pre = dict(res)
        image = {i + 1: res[i] for i in res}
        coeffs = [inner(image, older) for older in images]
        for c, p, q in zip(coeffs, directions, images):
            pre = axpy(pre, c, p)
            image = axpy(image, c, q)
        scale = 1.0 / jnp.sqrt(inner(image, image))
        pre = {i: pre[i] * scale for i in pre}
        image = {i: image[i] * scale for i in image}
        alpha = inner(res, image)
        field = axpy(field, -alpha, pre)
        res = axpy(res, alpha, image)
        norm_ref[step] = inner(res, res)[0, 0]
        directions.append(pre)
        images.append(image)
    x_ref[...] = field[0] * zs_ref[0] + field[1] * zs_ref[1] + field[2] * zs_ref[2]
    res_ref[...] = res[0] * r_ref[...] + res[1] * ws_ref[0] + res[2] * ws_ref[1] + res[3] * ws_ref[2]


def on_device(right_side, diagonal, horizontal, vertical, precond, edge_rows):
    rows, cols, levels = right_side.shape
    n_gx = lax.axis_size("gx")
    n_gy = lax.axis_size("gy")
    n_dev = n_gx * n_gy
    assert n_gx >= 4 and cols >= 3 and cols % 8 == 0
    high = rows * n_gy
    wide = cols + PAD
    cells = float(rows * cols * levels * n_dev)
    f32 = jnp.float32
    shaped = lambda *shape: jax.ShapeDtypeStruct(shape, f32)

    east_pack, west_pack = pl.pallas_call(
        pack_kernel,
        out_shape=(shaped(7, rows, levels),) * 2,
        in_specs=[VM] * 3,
        out_specs=(VM,) * 2,
        name="pack",
    )(right_side, diagonal, horizontal)
    ring = [(i, (i + 1) % n_gx) for i in range(n_gx)]
    from_west = lax.ppermute(east_pack, "gx", ring)
    from_east = lax.ppermute(west_pack, "gx", [(j, i) for i, j in ring])
    rw, dw, hw, last, initial, strips = pl.pallas_call(
        functools.partial(widen_kernel, n_gx=n_gx),
        out_shape=(shaped(rows, wide, levels),) * 3 + (shaped(7, wide, levels),) * 2 + (shaped(11, rows, levels),),
        in_specs=[VM] * 7,
        out_specs=(VM,) * 6,
        name="widen",
    )(right_side, diagonal, horizontal, east_pack, west_pack, from_east, from_west)
    line = [(i, i + 1) for i in range(n_gy - 1)]
    before = lax.ppermute(last, "gy", line)
    after = lax.ppermute(initial, "gy", [(j, i) for i, j in line])
    ag = lax.all_gather(strips, "gy")

    zs, ws, gram = pl.pallas_call(
        functools.partial(krylov_kernel, n_gx=n_gx),
        out_shape=(shaped(3, rows, cols, levels), shaped(3, rows, cols, levels), shaped(n_dev, 1, levels)),
        in_specs=[SM] + [VM] * 8,
        out_specs=(VM, VM, VM),
        scratch_shapes=[pltpu.VMEM((high, levels), f32)] * 4
        + [pltpu.VMEM((rows + 4, 1, levels), f32)],
        name="krylov",
    )(edge_rows, rw, dw, hw, before, after, ag, vertical[None], precond)

    parts = lax.all_to_all(gram, ("gx", "gy"), 0, 0)
    return pl.pallas_call(
        functools.partial(combine_kernel, cells=cells),
        out_shape=(
            jax.ShapeDtypeStruct((rows, cols, levels), f32),
            jax.ShapeDtypeStruct((rows, cols, levels), f32),
            jax.ShapeDtypeStruct((3,), f32),
        ),
        in_specs=[VM] * 4,
        out_specs=(VM, VM, SM),
        name="combine",
    )(parts, right_side, zs, ws)


def solution(mesh):
    in_specs = (P("gy", "gx", None), P("gy", "gx", None), P("gy", "gx", None), P(), P(), P())
    out_specs = (P("gy", "gx", None), P("gy", "gx", None), P())
    return jax.shard_map(
        on_device, mesh=mesh, in_specs=in_specs, out_specs=out_specs, check_vma=False
    )
```

```python
import functools

import jax
import jax.numpy as jnp
from jax import lax
from jax.experimental import pallas as pl
from jax.experimental.pallas import tpu as pltpu
from jax.sharding import PartitionSpec as P

PAD = 8
HI = lax.Precision.HIGHEST
VM = pl.BlockSpec(memory_space=pltpu.VMEM)
SM = pl.BlockSpec(memory_space=pltpu.SMEM)


def position(n_gx):
    gx = lax.axis_index("gx")
    half = n_gx // 2
    east = (gx == half - 1) | (gx == n_gx - 1)
    west = (gx == half) | (gx == 0)
    return gx, half, east, west


def pack_kernel(r_ref, d_ref, h_ref, east_ref, west_ref, last_ref, first_ref):
    rows, cols, _ = r_ref.shape
    slot = 0
    for ref, depth in ((r_ref, 3), (d_ref, 2), (h_ref, 2)):
        last_ref[slot : slot + depth] = ref[rows - depth :]
        first_ref[slot : slot + depth] = ref[:depth]
        for k in range(depth):
            east_ref[slot] = ref[:, cols - 1 - k, :]
            west_ref[slot] = ref[:, k, :]
            slot += 1


CORNER = ((0, 0), (1, 0), (0, 1), (3, 0), (5, 0))


def strip_kernel(east_own, west_own, east_ref, west_ref, strip_ref, *, n_gx):
    rows = east_ref.shape[1]
    _, _, seam_east, _ = position(n_gx)
    for place, k in enumerate((0, 1, 3, 5)):
        strip_ref[place] = jnp.where(seam_east, east_own[k], west_own[k])
    for k in range(7):
        strip_ref[4 + k] = jnp.where(seam_east, east_ref[k], west_ref[k])
    for side, ref in enumerate((east_ref, west_ref)):
        strip_ref[11 + side] = jnp.zeros_like(strip_ref[11 + side])
        for j, (slot, row) in enumerate(CORNER):
            strip_ref[11 + side, pl.ds(j, 1), :] = ref[slot, pl.ds(row, 1), :]
            strip_ref[11 + side, pl.ds(5 + j, 1), :] = ref[slot, pl.ds(rows - 1 - row, 1), :]


def krylov_kernel(edges, r_ref, d_ref, h_ref, east_ref, west_ref, before, after, ag, vert_ref, pc_ref,
                  zs_ref, ws_ref, gram_ref, n0_ref, o0_ref, gath_ref, cross_ref, halo_ref,
                  block_ref, dw_ref, hw_ref, *, n_gx):
    rows, cols, lev = r_ref.shape
    wide = cols + PAD
    n_gy = ag.shape[0]
    high = rows * n_gy
    first = lax.axis_index("gy") * rows
    gx, half, seam_east, seam_west = position(n_gx)
    table = jnp.where((gx == half - 1) | (gx == half), 0, 1)
    seam_col = jnp.where(seam_east, cols, jnp.where(seam_west, wide - 1, -1))
    panel = gx // half
    vert = vert_ref[...]
    m_own = pc_ref[panel]
    m_near = pc_ref[1 - panel]

    def mul(v, m):
        shape = v.shape
        out = lax.dot_general(v.reshape(-1, lev), m, (((1,), (1,)), ((), ())), precision=HI,
                              preferred_element_type=jnp.float32)
        return out.reshape(shape)

    def column_term(z):
        axis = z.ndim - 1
        lane = lax.broadcasted_iota(jnp.int32, z.shape, axis)
        up = jnp.where(lane == lev - 1, 0.0, pltpu.roll(z, lev - 1, axis))
        down = jnp.where(lane == 0, 0.0, pltpu.roll(z, 1, axis))
        return vert * (2.0 * z - up - down)

    def strip_apply(z, d, h, east, west):
        row = lax.broadcasted_iota(jnp.int32, z.shape, 0)
        north = jnp.where(row == high - 1, 0.0, pltpu.roll(z, high - 1, 0))
        south = jnp.where(row == 0, 0.0, pltpu.roll(z, 1, 0))
        return d * z + h * (4.0 * z - east - west - north - south) + column_term(z)

    def block_apply(z, d, h, depth):
        for k in range(rows + 2 * depth):
            y = jnp.clip(first - depth + k, 0, high - 1)
            halo_ref[k] = n0_ref[pl.ds(edges[table, y], 1), :]
        mid = z[1:-1]
        col = lax.broadcasted_iota(jnp.int32, mid.shape, 1)
        mid = jnp.where(col == seam_col, halo_ref[: rows + 2 * depth], mid)
        beside = pltpu.roll(mid, wide - 1, 1) + pltpu.roll(mid, 1, 1) + z[2:] + z[:-2]
        return d * mid + h * (4.0 * mid - beside) + column_term(mid)

    def strip(c):
        return jnp.concatenate([ag[g, c] for g in range(n_gy)], 0)

    def gather(source, target):
        def body(y, _):
            target[pl.ds(y, 1), :] = source[pl.ds(edges[table, y], 1), :]
            return 0
        lax.fori_loop(0, high, body, 0, unroll=16)

    gy = lax.axis_index("gy")
    sources = ((r_ref, block_ref, 3, 0), (d_ref, dw_ref, 2, 3), (h_ref, hw_ref, 2, 5))
    for ref, target, depth, slot in sources:
        target[:, cols:, :] = jnp.zeros((rows + 2 * depth, PAD, lev), jnp.float32)
        target[:depth, :cols, :] = before[slot : slot + depth]
        target[depth : depth + rows, :cols, :] = ref[...]
        target[depth + rows :, :cols, :] = after[slot : slot + depth]
        for k in range(depth):
            target[depth : depth + rows, cols + k, :] = east_ref[slot + k]
            target[depth : depth + rows, wide - 1 - k, :] = west_ref[slot + k]
    above = jnp.minimum(gy + 1, n_gy - 1)
    below = jnp.maximum(gy - 1, 0)
    places = ((block_ref, 3), (block_ref, 3), (block_ref, 3), (dw_ref, 2), (hw_ref, 2))
    for side in range(2):
        high_corner = jnp.where(gy + 1 < n_gy, ag[above, 11 + side], 0.0)
        low_corner = jnp.where(gy > 0, ag[below, 11 + side], 0.0)
        for j, (target, depth) in enumerate(places):
            slot, row = CORNER[j]
            step = slot if slot < 3 else 0
            col = cols + step if side == 0 else wide - 1 - step
            target[depth + rows + row, pl.ds(col, 1), :] = high_corner[j : j + 1]
            target[depth - 1 - row, pl.ds(col, 1), :] = low_corner[5 + j : 6 + j]
    block = block_ref[...]
    d = dw_ref[...]
    h = hw_ref[...]

    own = mul(jnp.stack([strip(0), strip(1)], 0), m_own)
    near = mul(jnp.stack([strip(4), strip(5), strip(6)], 0), m_near)
    n0_ref[...] = near[0]
    o0_ref[...] = own[0]
    gather(n0_ref, gath_ref)
    gather(o0_ref, cross_ref)
    z = mul(block, m_own)
    zs_ref[0] = z[3:-3, :cols]
    w_o0 = strip_apply(own[0], strip(2), strip(3), gath_ref[...], own[1])
    w_n0 = strip_apply(near[0], strip(7), strip(9), near[1], cross_ref[...])
    w_n1 = strip_apply(near[1], strip(8), strip(10), near[2], near[0])
    w = block_apply(z, d, h, 2)
    w0 = w[2:-2, :cols]
    ws_ref[0] = w0

    o0_ref[...] = mul(w_o0, m_own)
    near = mul(jnp.stack([w_n0, w_n1], 0), m_near)
    n0_ref[...] = near[0]
    gather(o0_ref, cross_ref)
    z = mul(w, m_own)
    zs_ref[1] = z[2:-2, :cols]
    w_n0 = strip_apply(near[0], strip(7), strip(9), near[1], cross_ref[...])
    w = block_apply(z, d[1:-1], h[1:-1], 1)
    w1 = w[1:-1, :cols]
    ws_ref[1] = w1

    n0_ref[...] = mul(w_n0, m_near)
    z = mul(w, m_own)
    zs_ref[2] = z[1:-1, :cols]
    w2 = block_apply(z, d[2:-2], h[2:-2], 0)[:, :cols]
    ws_ref[2] = w2

    vectors = (r_ref[...], w0, w1, w2)
    lane = lax.broadcasted_iota(jnp.int32, (1, lev), 1)
    row = jnp.zeros((1, lev), jnp.float32)
    count = 0
    for i in range(4):
        for j in range(i, 4):
            part = jnp.sum(vectors[i] * vectors[j], axis=0)
            part = jnp.sum(jnp.sum(part, axis=0, keepdims=True), axis=1, keepdims=True)
            row = jnp.where(lane == count, part, row)
            count += 1
    gram_ref[...] = jnp.broadcast_to(row[None], gram_ref.shape)


def combine_kernel(parts, r_ref, zs_ref, ws_ref, x_ref, res_ref, norm_ref, *, cells):
    total = jnp.sum(parts[...], axis=0) * (1.0 / cells)
    gram = {}
    count = 0
    for i in range(4):
        for j in range(i, 4):
            gram[i, j] = gram[j, i] = total[:, count : count + 1]
            count += 1

    def inner(a, b):
        out = None
        for i in a:
            for j in b:
                term = a[i] * b[j] * gram[i, j]
                out = term if out is None else out + term
        return out

    def axpy(a, c, b):
        out = dict(a)
        for i in b:
            out[i] = out[i] - c * b[i] if i in out else -c * b[i]
        return out

    one = jnp.ones((1, 1), jnp.float32)
    field = {}
    res = {0: one}
    directions = []
    images = []
    for step in range(3):
        pre = dict(res)
        image = {i + 1: res[i] for i in res}
        coeffs = [inner(image, older) for older in images]
        for c, p, q in zip(coeffs, directions, images):
            pre = axpy(pre, c, p)
            image = axpy(image, c, q)
        scale = 1.0 / jnp.sqrt(inner(image, image))
        pre = {i: pre[i] * scale for i in pre}
        image = {i: image[i] * scale for i in image}
        alpha = inner(res, image)
        field = axpy(field, -alpha, pre)
        res = axpy(res, alpha, image)
        norm_ref[step] = inner(res, res)[0, 0]
        directions.append(pre)
        images.append(image)
    x_ref[...] = field[0] * zs_ref[0] + field[1] * zs_ref[1] + field[2] * zs_ref[2]
    res_ref[...] = res[0] * r_ref[...] + res[1] * ws_ref[0] + res[2] * ws_ref[1] + res[3] * ws_ref[2]


def on_device(right_side, diagonal, horizontal, vertical, precond, edge_rows):
    rows, cols, levels = right_side.shape
    n_gx = lax.axis_size("gx")
    n_gy = lax.axis_size("gy")
    n_dev = n_gx * n_gy
    assert n_gx >= 4 and rows >= 10 and cols % 8 == 0
    high = rows * n_gy
    wide = cols + PAD
    cells = float(rows * cols * levels * n_dev)
    f32 = jnp.float32
    shaped = lambda *shape: jax.ShapeDtypeStruct(shape, f32)

    east_pack, west_pack, last, initial = pl.pallas_call(
        pack_kernel,
        out_shape=(shaped(7, rows, levels),) * 2 + (shaped(7, cols, levels),) * 2,
        in_specs=[VM] * 3,
        out_specs=(VM,) * 4,
        name="pack",
    )(right_side, diagonal, horizontal)
    ring = [(i, (i + 1) % n_gx) for i in range(n_gx)]
    from_west = lax.ppermute(east_pack, "gx", ring)
    from_east = lax.ppermute(west_pack, "gx", [(j, i) for i, j in ring])
    line = [(i, i + 1) for i in range(n_gy - 1)]
    before = lax.ppermute(last, "gy", line)
    after = lax.ppermute(initial, "gy", [(j, i) for i, j in line])
    strips = pl.pallas_call(
        functools.partial(strip_kernel, n_gx=n_gx),
        out_shape=shaped(13, rows, levels),
        in_specs=[VM] * 4,
        out_specs=VM,
        name="strips",
    )(east_pack, west_pack, from_east, from_west)
    ag = lax.all_gather(strips, "gy")

    zs, ws, gram = pl.pallas_call(
        functools.partial(krylov_kernel, n_gx=n_gx),
        out_shape=(shaped(3, rows, cols, levels), shaped(3, rows, cols, levels), shaped(n_dev, 1, levels)),
        in_specs=[SM] + [VM] * 10,
        out_specs=(VM, VM, VM),
        scratch_shapes=[pltpu.VMEM((high, levels), f32)] * 4
        + [
            pltpu.VMEM((rows + 4, 1, levels), f32),
            pltpu.VMEM((rows + 6, wide, levels), f32),
            pltpu.VMEM((rows + 4, wide, levels), f32),
            pltpu.VMEM((rows + 4, wide, levels), f32),
        ],
        name="krylov",
    )(edge_rows, right_side, diagonal, horizontal, from_east, from_west, before, after, ag, vertical[None], precond)

    parts = lax.all_to_all(gram, ("gx", "gy"), 0, 0)
    return pl.pallas_call(
        functools.partial(combine_kernel, cells=cells),
        out_shape=(
            jax.ShapeDtypeStruct((rows, cols, levels), f32),
            jax.ShapeDtypeStruct((rows, cols, levels), f32),
            jax.ShapeDtypeStruct((3,), f32),
        ),
        in_specs=[VM] * 4,
        out_specs=(VM, VM, SM),
        name="combine",
    )(parts, right_side, zs, ws)


def solution(mesh):
    in_specs = (P("gy", "gx", None), P("gy", "gx", None), P("gy", "gx", None), P(), P(), P())
    out_specs = (P("gy", "gx", None), P("gy", "gx", None), P())
    return jax.shard_map(
        on_device, mesh=mesh, in_specs=in_specs, out_specs=out_specs, check_vma=False
    )
```

```python
import functools

import jax
import jax.numpy as jnp
from jax import lax
from jax.experimental import pallas as pl
from jax.experimental.pallas import tpu as pltpu
from jax.sharding import PartitionSpec as P

PAD = 8
HELD_LIMIT = 2**21 + 2**19
HI = lax.Precision.HIGHEST
VM = pl.BlockSpec(memory_space=pltpu.VMEM)
SM = pl.BlockSpec(memory_space=pltpu.SMEM)


def position(n_gx):
    gx = lax.axis_index("gx")
    half = n_gx // 2
    east = (gx == half - 1) | (gx == n_gx - 1)
    west = (gx == half) | (gx == 0)
    return gx, half, east, west


def pack_kernel(r_ref, d_ref, h_ref, east_ref, west_ref, last_ref, first_ref):
    rows, cols, _ = r_ref.shape
    slot = 0
    for ref, depth in ((r_ref, 3), (d_ref, 2), (h_ref, 2)):
        last_ref[slot : slot + depth] = ref[rows - depth :]
        first_ref[slot : slot + depth] = ref[:depth]
        for k in range(depth):
            east_ref[slot] = ref[:, cols - 1 - k, :]
            west_ref[slot] = ref[:, k, :]
            slot += 1


CORNER = ((0, 0), (1, 0), (0, 1), (3, 0), (5, 0))


def strip_kernel(east_own, west_own, east_ref, west_ref, strip_ref, *, n_gx):
    rows = east_ref.shape[1]
    _, _, seam_east, _ = position(n_gx)
    for place, k in enumerate((0, 1, 3, 5)):
        strip_ref[place] = jnp.where(seam_east, east_own[k], west_own[k])
    for k in range(7):
        strip_ref[4 + k] = jnp.where(seam_east, east_ref[k], west_ref[k])
    for side, ref in enumerate((east_ref, west_ref)):
        strip_ref[11 + side] = jnp.zeros_like(strip_ref[11 + side])
        for j, (slot, row) in enumerate(CORNER):
            strip_ref[11 + side, pl.ds(j, 1), :] = ref[slot, pl.ds(row, 1), :]
            strip_ref[11 + side, pl.ds(5 + j, 1), :] = ref[slot, pl.ds(rows - 1 - row, 1), :]


def krylov_kernel(edges, r_ref, d_ref, h_ref, east_ref, west_ref, before, after, ag, vert_ref, pc_ref,
                  zs_ref, ws_ref, gram_ref, n0_ref, o0_ref, gath_ref, cross_ref, halo_ref,
                  block_ref, dw_ref, hw_ref, *, n_gx):
    rows, cols, lev = r_ref.shape
    wide = cols + PAD
    n_gy = ag.shape[0]
    high = rows * n_gy
    first = lax.axis_index("gy") * rows
    gx, half, seam_east, seam_west = position(n_gx)
    table = jnp.where((gx == half - 1) | (gx == half), 0, 1)
    seam_col = jnp.where(seam_east, cols, jnp.where(seam_west, wide - 1, -1))
    panel = gx // half
    vert = vert_ref[...]
    m_own = pc_ref[panel]
    m_near = pc_ref[1 - panel]

    def mul(v, m):
        shape = v.shape
        out = lax.dot_general(v.reshape(-1, lev), m, (((1,), (1,)), ((), ())), precision=HI,
                              preferred_element_type=jnp.float32)
        return out.reshape(shape)

    def column_term(z):
        axis = z.ndim - 1
        lane = lax.broadcasted_iota(jnp.int32, z.shape, axis)
        up = jnp.where(lane == lev - 1, 0.0, pltpu.roll(z, lev - 1, axis))
        down = jnp.where(lane == 0, 0.0, pltpu.roll(z, 1, axis))
        return vert * (2.0 * z - up - down)

    def strip_apply(z, d, h, east, west):
        row = lax.broadcasted_iota(jnp.int32, z.shape, 0)
        north = jnp.where(row == high - 1, 0.0, pltpu.roll(z, high - 1, 0))
        south = jnp.where(row == 0, 0.0, pltpu.roll(z, 1, 0))
        return d * z + h * (4.0 * z - east - west - north - south) + column_term(z)

    def block_apply(z, d, h, depth):
        for k in range(rows + 2 * depth):
            y = jnp.clip(first - depth + k, 0, high - 1)
            halo_ref[k] = n0_ref[pl.ds(edges[table, y], 1), :]
        mid = z[1:-1]
        col = lax.broadcasted_iota(jnp.int32, mid.shape, 1)
        mid = jnp.where(col == seam_col, halo_ref[: rows + 2 * depth], mid)
        beside = pltpu.roll(mid, wide - 1, 1) + pltpu.roll(mid, 1, 1) + z[2:] + z[:-2]
        return d * mid + h * (4.0 * mid - beside) + column_term(mid)

    def strip(c):
        return jnp.concatenate([ag[g, c] for g in range(n_gy)], 0)

    def gather(source, target):
        def body(y, _):
            target[pl.ds(y, 1), :] = source[pl.ds(edges[table, y], 1), :]
            return 0
        lax.fori_loop(0, high, body, 0, unroll=16)

    gy = lax.axis_index("gy")
    sources = ((r_ref, block_ref, 3, 0), (d_ref, dw_ref, 2, 3), (h_ref, hw_ref, 2, 5))
    for ref, target, depth, slot in sources:
        target[:, cols:, :] = jnp.zeros((rows + 2 * depth, PAD, lev), jnp.float32)
        target[:depth, :cols, :] = before[slot : slot + depth]
        target[depth : depth + rows, :cols, :] = ref[...]
        target[depth + rows :, :cols, :] = after[slot : slot + depth]
        for k in range(depth):
            target[depth : depth + rows, cols + k, :] = east_ref[slot + k]
            target[depth : depth + rows, wide - 1 - k, :] = west_ref[slot + k]
    above = jnp.minimum(gy + 1, n_gy - 1)
    below = jnp.maximum(gy - 1, 0)
    places = ((block_ref, 3), (block_ref, 3), (block_ref, 3), (dw_ref, 2), (hw_ref, 2))
    for side in range(2):
        high_corner = jnp.where(gy + 1 < n_gy, ag[above, 11 + side], 0.0)
        low_corner = jnp.where(gy > 0, ag[below, 11 + side], 0.0)
        for j, (target, depth) in enumerate(places):
            slot, row = CORNER[j]
            step = slot if slot < 3 else 0
            col = cols + step if side == 0 else wide - 1 - step
            target[depth + rows + row, pl.ds(col, 1), :] = high_corner[j : j + 1]
            target[depth - 1 - row, pl.ds(col, 1), :] = low_corner[5 + j : 6 + j]
    block = block_ref[...]
    d = dw_ref[...]
    h = hw_ref[...]

    own = mul(jnp.stack([strip(0), strip(1)], 0), m_own)
    near = mul(jnp.stack([strip(4), strip(5), strip(6)], 0), m_near)
    n0_ref[...] = near[0]
    o0_ref[...] = own[0]
    gather(n0_ref, gath_ref)
    gather(o0_ref, cross_ref)
    z = mul(block, m_own)
    zs_ref[0] = z[3:-3, :cols]
    w_o0 = strip_apply(own[0], strip(2), strip(3), gath_ref[...], own[1])
    w_n0 = strip_apply(near[0], strip(7), strip(9), near[1], cross_ref[...])
    w_n1 = strip_apply(near[1], strip(8), strip(10), near[2], near[0])
    w = block_apply(z, d, h, 2)
    w0 = w[2:-2, :cols]
    ws_ref[0] = w0

    o0_ref[...] = mul(w_o0, m_own)
    near = mul(jnp.stack([w_n0, w_n1], 0), m_near)
    n0_ref[...] = near[0]
    gather(o0_ref, cross_ref)
    z = mul(w, m_own)
    zs_ref[1] = z[2:-2, :cols]
    w_n0 = strip_apply(near[0], strip(7), strip(9), near[1], cross_ref[...])
    w = block_apply(z, d[1:-1], h[1:-1], 1)
    w1 = w[1:-1, :cols]
    ws_ref[1] = w1

    n0_ref[...] = mul(w_n0, m_near)
    z = mul(w, m_own)
    zs_ref[2] = z[1:-1, :cols]
    w2 = block_apply(z, d[2:-2], h[2:-2], 0)[:, :cols]
    ws_ref[2] = w2

    vectors = (r_ref[...], w0, w1, w2)
    lane = lax.broadcasted_iota(jnp.int32, (1, lev), 1)
    row = jnp.zeros((1, lev), jnp.float32)
    count = 0
    for i in range(4):
        for j in range(i, 4):
            part = jnp.sum(vectors[i] * vectors[j], axis=0)
            part = jnp.sum(jnp.sum(part, axis=0, keepdims=True), axis=1, keepdims=True)
            row = jnp.where(lane == count, part, row)
            count += 1
    gram_ref[...] = jnp.broadcast_to(row[None], gram_ref.shape)


def combine_kernel(parts, r_ref, zs_ref, ws_ref, x_ref, res_ref, norm_ref, *, cells):
    total = jnp.sum(parts[...], axis=0) * (1.0 / cells)
    gram = {}
    count = 0
    for i in range(4):
        for j in range(i, 4):
            gram[i, j] = gram[j, i] = total[:, count : count + 1]
            count += 1

    def inner(a, b):
        out = None
        for i in a:
            for j in b:
                term = a[i] * b[j] * gram[i, j]
                out = term if out is None else out + term
        return out

    def axpy(a, c, b):
        out = dict(a)
        for i in b:
            out[i] = out[i] - c * b[i] if i in out else -c * b[i]
        return out

    one = jnp.ones((1, 1), jnp.float32)
    field = {}
    res = {0: one}
    directions = []
    images = []
    for step in range(3):
        pre = dict(res)
        image = {i + 1: res[i] for i in res}
        coeffs = [inner(image, older) for older in images]
        for c, p, q in zip(coeffs, directions, images):
            pre = axpy(pre, c, p)
            image = axpy(image, c, q)
        scale = 1.0 / jnp.sqrt(inner(image, image))
        pre = {i: pre[i] * scale for i in pre}
        image = {i: image[i] * scale for i in image}
        alpha = inner(res, image)
        field = axpy(field, -alpha, pre)
        res = axpy(res, alpha, image)
        norm_ref[step] = inner(res, res)[0, 0]
        directions.append(pre)
        images.append(image)
    x_ref[...] = field[0] * zs_ref[0] + field[1] * zs_ref[1] + field[2] * zs_ref[2]
    res_ref[...] = res[0] * r_ref[...] + res[1] * ws_ref[0] + res[2] * ws_ref[1] + res[3] * ws_ref[2]


def on_device(right_side, diagonal, horizontal, vertical, precond, edge_rows):
    rows, cols, levels = right_side.shape
    n_gx = lax.axis_size("gx")
    n_gy = lax.axis_size("gy")
    n_dev = n_gx * n_gy
    assert n_gx >= 4 and rows >= 10 and cols % 8 == 0
    high = rows * n_gy
    wide = cols + PAD
    cells = float(rows * cols * levels * n_dev)
    f32 = jnp.float32
    held = 4 * levels * (6 * rows * cols + 13 * rows * (n_gy + 1) + 28 * (rows + cols))
    if held <= HELD_LIMIT:
        near = lambda x: pltpu.with_memory_space_constraint(x, pltpu.VMEM)
        shaped = lambda *shape: pltpu.VMEM(shape, f32)
    else:
        near = lambda x: x
        shaped = lambda *shape: jax.ShapeDtypeStruct(shape, f32)

    east_pack, west_pack, last, initial = pl.pallas_call(
        pack_kernel,
        out_shape=(shaped(7, rows, levels),) * 2 + (shaped(7, cols, levels),) * 2,
        in_specs=[VM] * 3,
        out_specs=(VM,) * 4,
        name="pack",
    )(right_side, diagonal, horizontal)
    ring = [(i, (i + 1) % n_gx) for i in range(n_gx)]
    from_west = lax.ppermute(east_pack, "gx", ring)
    from_east = lax.ppermute(west_pack, "gx", [(j, i) for i, j in ring])
    line = [(i, i + 1) for i in range(n_gy - 1)]
    before = lax.ppermute(last, "gy", line)
    after = lax.ppermute(initial, "gy", [(j, i) for i, j in line])
    strips = pl.pallas_call(
        functools.partial(strip_kernel, n_gx=n_gx),
        out_shape=shaped(13, rows, levels),
        in_specs=[VM] * 4,
        out_specs=VM,
        name="strips",
    )(*map(near, (east_pack, west_pack, from_east, from_west)))
    ag = lax.all_gather(strips, "gy")

    zs, ws, gram = pl.pallas_call(
        functools.partial(krylov_kernel, n_gx=n_gx),
        out_shape=(shaped(3, rows, cols, levels), shaped(3, rows, cols, levels), shaped(n_dev, 1, levels)),
        in_specs=[SM] + [VM] * 10,
        out_specs=(VM, VM, VM),
        scratch_shapes=[pltpu.VMEM((high, levels), f32)] * 4
        + [
            pltpu.VMEM((rows + 4, 1, levels), f32),
            pltpu.VMEM((rows + 6, wide, levels), f32),
            pltpu.VMEM((rows + 4, wide, levels), f32),
            pltpu.VMEM((rows + 4, wide, levels), f32),
        ],
        name="krylov",
    )(edge_rows, right_side, diagonal, horizontal, *map(near, (from_east, from_west, before, after, ag)), vertical[None], precond)

    parts = lax.all_to_all(gram, ("gx", "gy"), 0, 0)
    return pl.pallas_call(
        functools.partial(combine_kernel, cells=cells),
        out_shape=(
            jax.ShapeDtypeStruct((rows, cols, levels), f32),
            jax.ShapeDtypeStruct((rows, cols, levels), f32),
            jax.ShapeDtypeStruct((3,), f32),
        ),
        in_specs=[VM] * 4,
        out_specs=(VM, VM, SM),
        name="combine",
    )(near(parts), right_side, near(zs), near(ws))


def solution(mesh):
    in_specs = (P("gy", "gx", None), P("gy", "gx", None), P("gy", "gx", None), P(), P(), P())
    out_specs = (P("gy", "gx", None), P("gy", "gx", None), P())
    return jax.shard_map(
        on_device, mesh=mesh, in_specs=in_specs, out_specs=out_specs, check_vma=False
    )
```
